32 devices in a mesh: dp: 8 (over z, y), tensor: 4 (over x, core).
Axes of the slice: x: 2, y: 2, z: 4, core: 2. Of those that a mesh axis runs over, the one named last changes fastest.
Arguments:
- layer_input: bfloat16 [8192, 2048], P(('dp', 'tensor')), may hold values from -6 to 6
- first_gain: bfloat16 [2048], P('dp'), may hold values from 0.5 to 1.5
- first_shift: bfloat16 [2048], P('dp'), may hold values from -3 to 3
- query_weight: bfloat16 [2048, 2048], P('dp', 'tensor'), may hold values from -0.25 to 0.25
- query_bias: bfloat16 [16, 128], P('tensor', 'dp'), may hold values from -3 to 3
- keyval_weight: bfloat16 [2048, 256], P('dp'), may hold values from -0.125 to 0.125
- value_bias: bfloat16 [128], P('dp'), may hold values from -2 to 2
- out_weight: bfloat16 [2048, 2048], P('tensor', 'dp'), may hold values from -0.375 to 0.375
- out_bias: bfloat16 [2048], P('dp'), may hold values from -3 to 3
- second_gain: bfloat16 [2048], P('dp'), may hold values from 0.5 to 1.5
- second_shift: bfloat16 [2048], P('dp'), may hold values from -3 to 3
- up_weight: bfloat16 [2048, 8192], P('dp', 'tensor'), may hold values from -0.125 to 0.125
- up_bias: bfloat16 [64, 128], P('tensor', 'dp'), may hold values from -3 to 3
- down_weight: bfloat16 [8192, 2048], P('tensor', 'dp'), may hold values from -0.0625 to 0.0625
- down_bias: bfloat16 [2048], P('dp'), may hold values from -3 to 3
- grad_output: bfloat16 [8192, 2048], P(('dp', 'tensor')), may hold values from -6 to 6
Outputs:
- layer_output: bfloat16 [8192, 2048], P(('dp', 'tensor'))
- input_grad: float32 [8192, 2048], P(('dp', 'tensor'))
- grad_first_gain: float32 [2048], P('dp')
- grad_first_shift: float32 [2048], P('dp')
- grad_query_weight: float32 [2048, 2048], P('dp', 'tensor')
- grad_query_bias: float32 [16, 128], P('tensor', 'dp')
- grad_keyval_weight: float32 [2048, 256], P('dp')
- grad_value_bias: float32 [128], P('dp')
- grad_out_weight: float32 [2048, 2048], P('tensor', 'dp')
- grad_out_bias: float32 [2048], P('dp')
- grad_second_gain: float32 [2048], P('dp')
- grad_second_shift: float32 [2048], P('dp')
- grad_up_weight: float32 [2048, 8192], P('dp', 'tensor')
- grad_up_bias: float32 [64, 128], P('tensor', 'dp')
- grad_down_weight: float32 [8192, 2048], P('tensor', 'dp')
- grad_down_bias: float32 [2048], P('dp')
The draws below stay inside these ranges and needn't reach their ends.
All inputs are finite; a program needn't handle non-finite values.
Results may differ from the reference program's by a relative error of at most 0.024.
Values may be sent and summed in bfloat16 or wider, within the bound.
No kernel may reach another device: no remote copies, remote signals or barrier semaphores. Data moves between devices by JAX's collectives and lax.ppermute only.
A program may use at most 192 MiB of HBM per device.

```python
import jax
import jax.numpy as jnp
from jax import lax

D = 2048
H = 16
HD = 128
FF = 8192
LEN = 1024
TOKENS = 8192


def steps_of(rng, shape, cuts, least, top_value):
    def one(position, shards_of):
        draws = jax.random.uniform(jax.random.fold_in(jax.random.fold_in(rng, 6), position), (shards_of,), jnp.float32, least / len(cuts), top_value / len(cuts))
        return jnp.repeat(jnp.exp(draws), shape[position] // shards_of).reshape((-1,) + (1,) * (len(shape) - position - 1))

    loudness = one(*cuts[0])
    for cut in cuts[1:]:
        loudness = loudness * one(*cut)
    return loudness


def bell_draw(key, dims, scale, reach, shards=(), kind=jnp.bfloat16):
    drawn = scale * jax.random.normal(key, dims, jnp.float32)
    if shards:
        drawn = drawn * steps_of(key, dims, shards, -0.22, 0.18)
    return jnp.clip(drawn, -reach, reach).astype(kind)


def setup_inputs(seed: int = 0) -> dict:
    arg_keys = jax.random.split(jax.random.key(seed), 17)
    return {
        "layer_input": bell_draw(arg_keys[0], (TOKENS, D), 1.0, 6.0, ((0, 32),)),
        "first_gain": jnp.clip(1.0 + 0.1 * jax.random.normal(arg_keys[1], (D,), jnp.float32), 0.5, 1.5).astype(jnp.bfloat16),
        "first_shift": bell_draw(arg_keys[2], (D,), 0.3, 3.0, ((0, 8),)),
        "query_weight": bell_draw(arg_keys[3], (D, D), (D // 4) ** -0.5, 0.25, ((0, 8), (1, 4))),
        "query_bias": bell_draw(arg_keys[4], (H, HD), 0.5, 3.0, ((0, 4), (1, 8))),
        "keyval_weight": bell_draw(arg_keys[5], (D, 2 * HD), D ** -0.5, 0.125, ((0, 8),)),
        "value_bias": bell_draw(arg_keys[6], (HD,), 0.2, 2.0, ((0, 8),)),
        "out_weight": bell_draw(arg_keys[7], (D, D), (D // 8) ** -0.5, 0.375, ((0, 4), (1, 8))),
        "out_bias": bell_draw(arg_keys[8], (D,), 0.3, 3.0, ((0, 8),)),
        "second_gain": jnp.clip(1.0 + 0.1 * jax.random.normal(arg_keys[9], (D,), jnp.float32), 0.5, 1.5).astype(jnp.bfloat16),
        "second_shift": bell_draw(arg_keys[10], (D,), 0.3, 3.0, ((0, 8),)),
        "up_weight": bell_draw(arg_keys[11], (D, FF), D ** -0.5, 0.125, ((0, 8), (1, 4))),
        "up_bias": bell_draw(arg_keys[12], (FF // HD, HD), 0.5, 3.0, ((0, 4), (1, 8))),
        "down_weight": bell_draw(arg_keys[13], (FF, D), FF ** -0.5, 0.0625, ((0, 4), (1, 8))),
        "down_bias": bell_draw(arg_keys[14], (D,), 0.3, 3.0, ((0, 8),)),
        "grad_output": bell_draw(arg_keys[15], (TOKENS, D), 1.0, 6.0, ((0, 32),)),
    }


@jax.custom_vjp
def low(v):
    return lax.optimization_barrier(v.astype(jnp.bfloat16)).astype(jnp.float32)

@jax.custom_vjp
def low_back(v):
    return v

def low_keep(v):
    return (low(v), None)

def low_pass(kept, grad):
    return (grad,)

def back_keep(v):
    return (v, None)

def back_low(kept, grad):
    return (low(grad),)
low.defvjp(low_keep, low_pass)
low_back.defvjp(back_keep, back_low)
EPS = 1e-05
HIGH = lax.Precision.HIGHEST

def layer_norm(rows, gain, shift):
    mean = lax.optimization_barrier(jnp.mean(rows, axis=-1, keepdims=True))
    centred = rows - mean
    spread = lax.optimization_barrier(jnp.mean(centred * centred, axis=-1, keepdims=True))
    return centred * lax.rsqrt(spread + EPS) * gain + shift

def gelu_tanh(value):
    return jax.nn.gelu(value, approximate=True)

def attention(query, keys, values):
    length = keys.shape[0]
    block = min(512, length)
    count = length // block
    scale = HD ** (-0.5)
    blocks = query.reshape(count, block, H, HD)
    starts = jnp.arange(count, dtype=jnp.int32) * block

    def one_block(pair):
        piece, start = pair
        scores = jnp.einsum('bhe,ke->hbk', piece, keys, precision=HIGH) * scale
        scores = low_back(scores)
        rows = start + jnp.arange(block, dtype=jnp.int32)[:, None]
        columns = jnp.arange(length, dtype=jnp.int32)[None, :]
        masked = jnp.where(columns <= rows, scores, -1e+30)
        probs = low(jax.nn.softmax(masked, axis=-1))
        return jnp.einsum('hbk,ke->bhe', probs, values, precision=HIGH)
    heads = lax.map(jax.checkpoint(one_block), (blocks, starts))
    return heads.reshape(length, H * HD)

def layer(sequence, params):
    first_gain, first_shift, query_weight, query_bias, keyval_weight, value_bias, out_weight, out_bias, second_gain, second_shift, up_weight, up_bias, down_weight, down_bias = params
    normed = low(layer_norm(sequence, first_gain, first_shift))
    query = low_back(low(jnp.dot(normed, query_weight, precision=HIGH) + query_bias.reshape(-1)))
    keyval = jnp.dot(normed, keyval_weight, precision=HIGH)
    keys = low_back(low(keyval[:, :HD]))
    values = low_back(low(keyval[:, HD:] + value_bias))
    mixed = low_back(low(attention(query, keys, values)))
    attn = low_back(jnp.dot(mixed, out_weight, precision=HIGH))
    resid = sequence + attn + out_bias
    normed_second = low(layer_norm(resid, second_gain, second_shift))
    upper = low_back(jnp.dot(normed_second, up_weight, precision=HIGH) + up_bias.reshape(-1))
    active = low(gelu_tanh(upper))
    branch = low_back(jnp.dot(active, down_weight, precision=HIGH))
    return resid + branch + down_bias

def reference(layer_input, first_gain, first_shift, query_weight, query_bias, keyval_weight, value_bias, out_weight, out_bias, second_gain, second_shift, up_weight, up_bias, down_weight, down_bias, grad_output):
    params = tuple((p.astype(jnp.float32) for p in (first_gain, first_shift, query_weight, query_bias, keyval_weight, value_bias, out_weight, out_bias, second_gain, second_shift, up_weight, up_bias, down_weight, down_bias)))
    inputs = layer_input.astype(jnp.float32).reshape(-1, LEN, D)
    cotangents = grad_output.astype(jnp.float32).reshape(-1, LEN, D)

    def one_sequence(totals, pair):
        sequence, cotangent = pair
        result, pullback = jax.vjp(layer, sequence, params)
        grad_sequence, grad_params = pullback(cotangent)
        totals = jax.tree.map(lambda left, right: left + right, totals, grad_params)
        return (totals, (result, grad_sequence))
    zeros = tuple((jnp.zeros(p.shape, jnp.float32) for p in params))
    totals, (results, grads) = lax.scan(one_sequence, zeros, (inputs, cotangents))
    return (results.reshape(-1, D).astype(jnp.bfloat16), grads.reshape(-1, D), totals[0], totals[1], totals[2], totals[3], totals[4], totals[5], totals[6], totals[7], totals[8], totals[9], totals[10], totals[11], totals[12], totals[13])
```

```python
import jax
import jax.numpy as jnp
from jax import lax
from jax.sharding import PartitionSpec as P

EPS = 1e-05
MASKED = -1e30
F32 = jnp.float32
BF16 = jnp.bfloat16
CHUNKS = 2


def stages_of(size):
    stages = []
    rest = size
    while rest > 1:
        radix = 4 if rest % 4 == 0 and rest > 4 else 2
        rest //= radix
        stages.append((rest, radix))
    return stages


def masks_of(size):
    order = [0]
    for stride, radix in stages_of(size):
        order = [mask ^ (k * stride) for k in range(radix) for mask in order]
    return order


def swap(array, axis_name, size, mask):
    return lax.ppermute(array, axis_name, [(i, i ^ mask) for i in range(size)])


def gather(array, axis_name, size, dim):
    current = array
    for stride, radix in stages_of(size):
        parts = [current]
        for k in range(1, radix):
            parts.append(swap(current, axis_name, size, k * stride))
        current = jnp.concatenate(parts, axis=dim)
    return current


def scatter(array, axis_name, size, dim):
    current = array
    for stride, radix in reversed(stages_of(size)):
        parts = jnp.split(current.astype(BF16), radix, axis=dim)
        total = parts[0].astype(F32)
        for k in range(1, radix):
            total = total + swap(parts[k], axis_name, size, k * stride).astype(F32)
        current = total
    return current


def total_of(array, axis_name, size):
    current = array
    mask = 1
    while mask < size:
        sent = current.astype(BF16)
        current = sent.astype(F32) + swap(sent, axis_name, size, mask).astype(F32)
        mask *= 2
    return current


def cross(left, right):
    return lax.dot_general(
        left, right, (((0,), (0,)), ((), ())), preferred_element_type=F32
    )


def against(left, right):
    return lax.dot_general(
        left, right, (((1,), (1,)), ((), ())), preferred_element_type=F32
    )


def dot(left, right):
    return jnp.dot(left, right, preferred_element_type=F32)


def norm_stats(rows):
    mean = jnp.mean(rows, axis=-1, keepdims=True)
    centred = rows - mean
    spread = jnp.mean(centred * centred, axis=-1, keepdims=True)
    scale = lax.rsqrt(spread + EPS)
    return centred * scale, scale


def norm_back(grad, unit, scale, gain):
    scaled = grad * gain
    first = jnp.mean(scaled, axis=-1, keepdims=True)
    second = jnp.mean(scaled * unit, axis=-1, keepdims=True)
    return scale * (scaled - first - unit * second)


def gelu_tanh(value):
    return jax.nn.gelu(value, approximate=True)


def softmax_block(piece, keys, rows, columns, scale):
    scores = jnp.einsum("bhe,ke->hbk", piece, keys, preferred_element_type=F32) * scale
    masked = jnp.where(columns[None, None, :] <= rows[None, :, None], scores, MASKED)
    highest = jnp.max(masked, axis=-1, keepdims=True)
    powers = jnp.exp(masked - highest)
    return powers / jnp.sum(powers, axis=-1, keepdims=True)


def head_blocks(array, width, block):
    return array.reshape(array.shape[0] // block, block, array.shape[1] // width, width)


def attend(query, keys, values, places, block):
    width = keys.shape[1]
    scale = width ** (-0.5)
    mixed = []
    for index, piece in enumerate(head_blocks(query, width, block)):
        rows = places[index * block : (index + 1) * block]
        probs = softmax_block(piece, keys, rows, places, scale).astype(BF16)
        mixed.append(jnp.einsum("hbk,ke->bhe", probs, values, preferred_element_type=F32))
    return jnp.concatenate(mixed, axis=0).reshape(query.shape)


def attend_back(query, keys, values, grad_mixed, places, block):
    width = keys.shape[1]
    scale = width ** (-0.5)
    key_grad = jnp.zeros(keys.shape, F32)
    value_grad = jnp.zeros(keys.shape, F32)
    query_grads = []
    pieces = head_blocks(query, width, block)
    grad_pieces = head_blocks(grad_mixed, width, block)
    for index in range(pieces.shape[0]):
        piece, grad_piece = pieces[index], grad_pieces[index]
        rows = places[index * block : (index + 1) * block]
        probs = softmax_block(piece, keys, rows, places, scale)
        grad_probs = jnp.einsum("bhe,ke->hbk", grad_piece, values, preferred_element_type=F32)
        inner = jnp.sum(probs * grad_probs, axis=-1, keepdims=True)
        grad_scores = (probs * (grad_probs - inner)).astype(BF16)
        query_grads.append(
            jnp.einsum("hbk,ke->bhe", grad_scores, keys, preferred_element_type=F32) * scale
        )
        key_grad = key_grad + scale * jnp.einsum(
            "hbk,bhe->ke", grad_scores, piece, preferred_element_type=F32
        )
        value_grad = value_grad + jnp.einsum(
            "hbk,bhe->ke", probs.astype(BF16), grad_piece, preferred_element_type=F32
        )
    query_grad = jnp.concatenate(query_grads, axis=0).reshape(query.shape)
    return query_grad, key_grad, value_grad


def make_shards(dp, tensor):
    dp_masks = masks_of(dp)
    tensor_masks = masks_of(tensor)

    def dp_gather(array, dim):
        return gather(array, "dp", dp, dim)

    def dp_scatter(array, dim):
        return scatter(array, "dp", dp, dim)

    def row_gather(array):
        return gather(array, "tensor", tensor, 0)

    def row_scatter(array):
        return scatter(array, "tensor", tensor, 0)

    def shards(
        layer_input,
        first_gain,
        first_shift,
        query_weight,
        query_bias,
        keyval_weight,
        value_bias,
        out_weight,
        out_bias,
        second_gain,
        second_shift,
        up_weight,
        up_bias,
        down_weight,
        down_bias,
        grad_output,
    ):
        me = lax.axis_index("dp")
        seat = lax.axis_index("tensor")
        local_rows, width_all = layer_input.shape
        part = width_all // dp
        heads = query_bias.shape[0]
        head_part = query_bias.shape[1]
        width = head_part * dp
        hidden = up_weight.shape[1]
        step = hidden // CHUNKS

        def to_order(array):
            return jnp.concatenate(
                [
                    lax.dynamic_slice_in_dim(array, (me ^ mask) * part, part, 1)
                    for mask in dp_masks
                ],
                axis=1,
            )

        place_of = jnp.asarray([dp_masks.index(m) for m in range(dp)], jnp.int32)

        def from_order(array):
            return jnp.concatenate(
                [
                    lax.dynamic_slice_in_dim(array, place_of[me ^ j] * part, part, 1)
                    for j in range(dp)
                ],
                axis=1,
            )

        ids = jnp.asarray(dp_masks, jnp.int32)
        pick = (jnp.arange(dp, dtype=jnp.int32)[:, None] == (ids ^ me)[None, :]).astype(BF16)

        def true_blocks(blocks):
            return jnp.dot(pick, blocks, preferred_element_type=F32).astype(blocks.dtype)

        def order_blocks(blocks):
            return jnp.dot(pick.T, blocks, preferred_element_type=F32).astype(blocks.dtype)

        inputs_bf = to_order(layer_input)
        cotangent_bf = to_order(grad_output)
        inputs_all = row_gather(inputs_bf)

        vectors = jnp.concatenate(
            [
                first_gain,
                first_shift,
                out_bias,
                second_gain,
                second_shift,
                down_bias,
                query_bias.reshape(-1),
                up_bias.reshape(-1),
                value_bias,
            ]
        )[None, :]
        vectors_all = dp_gather(vectors, 0).reshape(dp, -1)
        def feature(index):
            return vectors_all[:, index * part : (index + 1) * part].reshape(-1).astype(F32)

        gain_one, shift_one, out_shift, gain_two, shift_two, down_shift = (
            feature(i) for i in range(6)
        )
        rest = true_blocks(vectors_all[:, 6 * part :])
        q_size = query_bias.size
        u_size = up_bias.size
        query_shift = (
            rest[:, :q_size].reshape(dp, heads, head_part).transpose(1, 0, 2).reshape(-1).astype(F32)
        )
        up_rows = up_bias.shape[0]
        up_shift = (
            rest[:, q_size : q_size + u_size]
            .reshape(dp, up_rows, up_bias.shape[1])
            .transpose(1, 0, 2)
            .reshape(-1)
            .astype(F32)
        )
        value_shift = rest[:, q_size + u_size :].reshape(-1).astype(F32)

        qkv_full = dp_gather(jnp.concatenate([query_weight, keyval_weight], axis=1), 0)
        out_full = dp_gather(out_weight, 1)
        up_full = []
        down_full = []
        for c in range(CHUNKS):
            up_full.append(dp_gather(up_weight[:, c * step : (c + 1) * step], 0))
            down_full.append(dp_gather(down_weight[c * step : (c + 1) * step], 1))
        cotangent_all = row_gather(cotangent_bf)

        unit_all, unused = norm_stats(inputs_all.astype(F32))
        normed_all = (unit_all * gain_one + shift_one).astype(BF16)
        joined = dot(normed_all, qkv_full)
        q_width = heads * width
        query = (joined[:, :q_width] + query_shift).astype(BF16)
        keys = joined[:, q_width : q_width + width].astype(BF16)
        values = (joined[:, q_width + width :] + value_shift).astype(BF16)
        length = local_rows * tensor
        places = jnp.concatenate(
            [
                jnp.arange(local_rows, dtype=jnp.int32) + (seat ^ mask) * local_rows
                for mask in tensor_masks
            ]
        )
        block = min(512, length)
        mixed = attend(query, keys, values, places, block).astype(BF16)
        attn = row_scatter(dot(mixed, out_full))
        inputs = inputs_bf.astype(F32)
        resid = inputs + attn + out_shift

        unit_two, scale_two = norm_stats(resid)
        second = (unit_two * gain_two + shift_two).astype(BF16)
        second_all = row_gather(second)
        uppers = []
        actives = []
        down_grads = []
        up_grads = []
        grad_uppers = []
        branch = None
        grad_second = None
        for c in range(CHUNKS):
            upper = dot(second_all, up_full[c]) + up_shift[c * step : (c + 1) * step]
            active = gelu_tanh(upper).astype(BF16)
            down_grads.append(dp_scatter(cross(active, cotangent_all), 1))
            grad_active = against(cotangent_all, down_full[c])
            unused_value, gelu_pull = jax.vjp(gelu_tanh, upper)
            grad_upper = gelu_pull(grad_active)[0].astype(BF16)
            grad_uppers.append(grad_upper)
            up_grads.append(dp_scatter(cross(second_all, grad_upper), 0))
            actives.append(active)
        active_all = jnp.concatenate(actives, axis=1)
        grad_upper_all = jnp.concatenate(grad_uppers, axis=1)
        grad_second = row_scatter(against(grad_upper_all, jnp.concatenate(up_full, axis=1)))
        branch = row_scatter(dot(active_all, jnp.concatenate(down_full, axis=0)))
        output = resid + branch + down_shift
        layer_output = from_order(output.astype(BF16))

        cotangent = cotangent_bf.astype(F32)
        grad_up_shift = jnp.sum(grad_upper_all, axis=0, dtype=F32)
        grad_gain_two = jnp.sum(grad_second * unit_two, axis=0)
        grad_shift_two = jnp.sum(grad_second, axis=0)
        grad_resid = cotangent + norm_back(grad_second, unit_two, scale_two, gain_two)

        resid_all = row_gather(grad_resid.astype(BF16))
        grad_out = dp_scatter(cross(mixed, resid_all), 1)
        grad_mixed = against(resid_all, out_full).astype(BF16)
        grad_query, grad_keys, grad_values = attend_back(
            query, keys, values, grad_mixed, places, block
        )
        grad_query = grad_query.astype(BF16)
        grad_query_shift = jnp.sum(grad_query, axis=0, dtype=F32)
        from_query = row_scatter(against(grad_query, qkv_full[:, :q_width]))
        keyval_part = jnp.concatenate([grad_keys, grad_values], axis=1)
        grad_keyval = row_scatter(keyval_part).astype(BF16)
        keyval_all = row_gather(grad_keyval)
        grad_query_weight = dp_scatter(cross(normed_all, grad_query), 0)
        share = 2 * width // tensor
        keyval_mine = lax.dynamic_slice_in_dim(keyval_all, seat * share, share, 1)
        keyval_block = dp_scatter(cross(normed_all, keyval_mine), 0)
        keyval_blocks = row_gather(keyval_block[None])
        shares = jnp.asarray(tensor_masks, jnp.int32) ^ seat
        grad_keyval_weight = jnp.zeros((part, tensor, share), F32)
        for p in range(tensor):
            grad_keyval_weight = lax.dynamic_update_slice(
                grad_keyval_weight, keyval_blocks[p][:, None, :], (0, shares[p], 0)
            )
        grad_keyval_weight = grad_keyval_weight.reshape(part, tensor * share)
        grad_normed = from_query + against(grad_keyval, qkv_full[:, q_width:])
        unit_one, scale_one = norm_stats(inputs)
        grad_gain_one = jnp.sum(grad_normed * unit_one, axis=0)
        grad_shift_one = jnp.sum(grad_normed, axis=0)
        input_grad = from_order(
            grad_resid + norm_back(grad_normed, unit_one, scale_one, gain_one)
        )

        row_sums = jnp.stack(
            [
                grad_gain_one,
                grad_shift_one,
                jnp.sum(grad_resid, axis=0),
                grad_gain_two,
                grad_shift_two,
                jnp.sum(cotangent, axis=0),
            ]
        )
        value_sum = jnp.sum(grad_keyval[:, width:], axis=0, dtype=F32)
        shared = jnp.concatenate([row_sums.reshape(-1), value_sum])
        shared = total_of(shared, "tensor", tensor)
        row_sums = shared[: 6 * width_all].reshape(6, dp, part).transpose(1, 0, 2).reshape(dp, -1)
        value_blocks = shared[6 * width_all :].reshape(dp, -1)
        query_blocks = (
            grad_query_shift.reshape(heads, dp, head_part).transpose(1, 0, 2).reshape(dp, -1)
        )
        up_blocks = (
            grad_up_shift.reshape(up_rows, dp, up_bias.shape[1]).transpose(1, 0, 2).reshape(dp, -1)
        )
        true_order = jnp.concatenate([query_blocks, up_blocks, value_blocks], axis=1).astype(BF16)
        packed = jnp.concatenate([row_sums.astype(BF16), order_blocks(true_order)], axis=1)
        summed = dp_scatter(packed, 0)[0]
        sums = [summed[i * part : (i + 1) * part] for i in range(6)]
        tail = summed[6 * part :]
        return (
            layer_output,
            input_grad,
            sums[0],
            sums[1],
            grad_query_weight,
            tail[:q_size].reshape(heads, head_part),
            grad_keyval_weight,
            tail[q_size + u_size :],
            grad_out,
            sums[2],
            sums[3],
            sums[4],
            jnp.concatenate(up_grads, axis=1),
            tail[q_size : q_size + u_size].reshape(up_bias.shape),
            jnp.concatenate(down_grads, axis=0),
            sums[5],
        )

    return shards


def solution(mesh):
    in_specs = (
        P(("dp", "tensor"), None),
        P("dp"),
        P("dp"),
        P("dp", "tensor"),
        P("tensor", "dp"),
        P("dp", None),
        P("dp"),
        P("tensor", "dp"),
        P("dp"),
        P("dp"),
        P("dp"),
        P("dp", "tensor"),
        P("tensor", "dp"),
        P("tensor", "dp"),
        P("dp"),
        P(("dp", "tensor"), None),
    )
    out_specs = (
        P(("dp", "tensor"), None),
        P(("dp", "tensor"), None),
        P("dp"),
        P("dp"),
        P("dp", "tensor"),
        P("tensor", "dp"),
        P("dp", None),
        P("dp"),
        P("tensor", "dp"),
        P("dp"),
        P("dp"),
        P("dp"),
        P("dp", "tensor"),
        P("tensor", "dp"),
        P("tensor", "dp"),
        P("dp"),
    )
    shards = make_shards(mesh.shape["dp"], mesh.shape["tensor"])
    return jax.shard_map(shards, mesh=mesh, in_specs=in_specs, out_specs=out_specs, check_vma=False)
```
